32 devices in a mesh: dp: 8 (over z, core), tp: 4 (over y, x).
Axes of the slice: x: 2, y: 2, z: 4, core: 2. Of those that a mesh axis runs over, the one named last changes fastest.
Arguments:
- layer_input: float32 [16384, 2048], P(('dp', 'tp')), may hold values from -6 to 6
- lengths: int32 [12], replicated, may hold values from 1024 to 2048, as said below
- row_owner: int32 [12], replicated, may hold values from 0 to 7, as said below
- norm_gain1: float32 [2048], replicated, may hold values from 0.25 to 1.75
- w_query: bfloat16 [2048, 256], P(None, 'tp'), may hold values from -0.125 to 0.125
- w_key: bfloat16 [2048, 256], P(None, 'tp'), may hold values from -0.125 to 0.125
- w_value: bfloat16 [2048, 2048], P(None, 'tp'), may hold values from -0.125 to 0.125
- w_out: bfloat16 [2048, 2048], P('tp'), may hold values from -1.5 to 1.5
- norm_gain2: float32 [2048], replicated, may hold values from 0.25 to 1.75
- w_gate: bfloat16 [2048, 5504], P(None, 'tp'), may hold values from -0.125 to 0.125
- w_up: bfloat16 [2048, 5504], P(None, 'tp'), may hold values from -0.125 to 0.125
- w_down: bfloat16 [5504, 2048], P('tp'), may hold values from -0.078125 to 0.078125
- cotangent: float32 [16384, 2048], P(('dp', 'tp')), may hold values from -6 to 6
Outputs:
- output: float32 [16384, 2048], P(('dp', 'tp'))
- input_grad: float32 [16384, 2048], P(('dp', 'tp'))
- gain1_grad: float32 [2048], replicated
- query_grad: float32 [2048, 256], P('dp', 'tp')
- key_grad: float32 [2048, 256], P('dp', 'tp')
- value_grad: float32 [2048, 2048], P('dp', 'tp')
- out_grad: float32 [2048, 2048], P('tp', 'dp')
- gain2_grad: float32 [2048], replicated
- gate_grad: float32 [2048, 5504], P('dp', 'tp')
- up_grad: float32 [2048, 5504], P('dp', 'tp')
- down_grad: float32 [5504, 2048], P('tp', 'dp')
The draws below stay inside these ranges and needn't reach their ends.
Inputs may be any that keep to these rules, and one draw needn't show every extreme that they name: `lengths`: every row is 2048 or 1024 tokens long; the rows of one group fill exactly its 2048 places; half of the groups hold one row and the other half two. `row_owner`: every group holds at least one row.
All inputs are finite; a program needn't handle non-finite values.
Results may differ from the reference program's by a relative error of at most 0.019.
Values may be sent and summed in bfloat16 or wider, within the bound.
A program may use at most 256 MiB of HBM per device.

```python
import math
import jax
import jax.numpy as jnp
from jax import lax

D = 2048
HEADS = 16
FEAT = 16
HV = 128
FF = 5504
BLOCK = 512
GROUP_TOK = 2048
TOKENS = 16384
ROWS = 12
N_DP = 8


def packing(key):
    half = N_DP // 2
    groups = jax.random.permutation(jax.random.fold_in(key, 7), N_DP).astype(jnp.int32)
    owners = jnp.concatenate([groups[:half], groups[half:], groups[half:]])
    sizes = jnp.concatenate([jnp.full((half,), GROUP_TOK, jnp.int32), jnp.full((2 * (N_DP - half),), GROUP_TOK // 2, jnp.int32)])
    shuffle = jax.random.permutation(jax.random.fold_in(key, 9), ROWS).astype(jnp.int32)
    return (sizes[shuffle], owners[shuffle])


def draw_lengths(key, part):
    return packing(key)[0]


def draw_row_owner(key, part):
    return packing(key)[1]


def strengthened(drawn, rng, source, target, parts, factor):
    def block_of(position):
        return (jnp.arange(drawn.shape[position]) // (drawn.shape[position] // parts)).reshape((-1,) + (1,) * (drawn.ndim - 1 - position))

    one_side = jax.random.permutation(rng, parts)[block_of(target)]
    far = (block_of(target) + parts // 2) % parts
    return jnp.where((block_of(source) == one_side) | (block_of(source) == far), factor * drawn, drawn)


def levels(key, dims, pieces, smallest, high):
    def one(dim, shards_of):
        draws = jax.random.uniform(jax.random.fold_in(jax.random.fold_in(key, 6), dim), (shards_of,), jnp.float32, smallest / len(pieces), high / len(pieces))
        return jnp.repeat(jnp.exp(draws), dims[dim] // shards_of).reshape((-1,) + (1,) * (len(dims) - dim - 1))

    loudness = one(*pieces[0])
    for cut in pieces[1:]:
        loudness = loudness * one(*cut)
    return loudness


def normal_values(rng, dims, scale, limit, split=(), kind=jnp.bfloat16):
    values = scale * jax.random.normal(rng, dims, jnp.float32)
    if split:
        values = values * levels(rng, dims, split, -0.22, 0.18)
    return jnp.clip(values, -limit, limit).astype(kind)


def gaussian_with(key, extent, deviation, most, shards, heavy, kind=jnp.bfloat16):
    values = deviation * jax.random.normal(key, extent, jnp.float32)
    if shards:
        values = values * levels(key, extent, shards, -0.22, 0.18)
    return jnp.clip(strengthened(values, jax.random.fold_in(key, 3), *heavy), -most, most).astype(kind)


def setup_inputs(seed: int = 0) -> dict:
    arg_keys = jax.random.split(jax.random.key(seed), 14)
    layer_input = normal_values(arg_keys[0], (TOKENS, D), 1.0, 6.0, ((0, 32),), jnp.float32)
    lengths = draw_lengths(jax.random.fold_in(arg_keys[13], 71), 0)
    row_owner = draw_row_owner(jax.random.fold_in(arg_keys[13], 71), 0)
    norm_gain1 = jnp.clip(1.0 + 0.15 * jax.random.normal(arg_keys[3], (D,), jnp.float32), 0.25, 1.75)
    w_query = normal_values(arg_keys[4], (D, HEADS * FEAT), D ** -0.5, 0.125, ((1, 4),))
    w_key = normal_values(arg_keys[5], (D, HEADS * FEAT), D ** -0.5, 0.125, ((1, 4),))
    w_value = normal_values(arg_keys[6], (D, HEADS * HV), D ** -0.5, 0.125, ((1, 4),))
    w_out = normal_values(arg_keys[7], (HEADS * HV, D), 16 ** -0.5, 1.5, ((0, 4),))
    norm_gain2 = jnp.clip(1.0 + 0.15 * jax.random.normal(arg_keys[8], (D,), jnp.float32), 0.25, 1.75)
    w_gate = normal_values(arg_keys[9], (D, FF), D ** -0.5, 0.125, ((1, 4),))
    w_up = normal_values(arg_keys[10], (D, FF), D ** -0.5, 0.125, ((1, 4),))
    w_down = normal_values(arg_keys[11], (FF, D), FF ** -0.5, 0.078125, ((0, 4),))
    cotangent = gaussian_with(arg_keys[12], (TOKENS, D), 1.0, 6.0, ((0, 32),), (0, 1, 32, 2.75), jnp.float32)
    return {"layer_input": layer_input, "lengths": lengths, "row_owner": row_owner, "norm_gain1": norm_gain1, "w_query": w_query, "w_key": w_key, "w_value": w_value, "w_out": w_out, "norm_gain2": norm_gain2, "w_gate": w_gate, "w_up": w_up, "w_down": w_down, "cotangent": cotangent}


EPS = 1e-05
HIGHEST = lax.Precision.HIGHEST

@jax.custom_vjp
def low(v):
    return lax.optimization_barrier(v.astype(jnp.bfloat16)).astype(jnp.float32)

@jax.custom_vjp
def low_back(v):
    return v

def low_keep(v):
    return (low(v), None)

def low_pass(kept, grad):
    return (grad,)

def back_keep(v):
    return (v, None)

def back_low(kept, grad):
    return (low(grad),)
low.defvjp(low_keep, low_pass)
low_back.defvjp(back_keep, back_low)

def matmul(left, right):
    return jnp.dot(left, right, precision=HIGHEST)

def root_norm(values, gain):
    return values * lax.rsqrt(lax.optimization_barrier(jnp.mean(values * values, axis=-1, keepdims=True)) + EPS) * gain

def taylor_features(rows):
    columns = rows.T
    width = columns.shape[0]
    outer = (columns[:, None, :] * columns[None, :, :]).reshape(width * width, columns.shape[1])
    ones = jnp.ones((1, columns.shape[1]), columns.dtype)
    return jnp.concatenate([ones, columns / math.sqrt(math.sqrt(width)), outer / (math.sqrt(2.0) * math.sqrt(width))], axis=0)

def segment_numbers(lengths, row_owner, group, total):
    order = jnp.arange(lengths.shape[0], dtype=jnp.int32)
    same = row_owner[:, None] == row_owner[None, :]
    before = same & (order[None, :] < order[:, None])
    offset = lax.optimization_barrier(jnp.sum(jnp.where(before, lengths[None, :], 0), axis=1, dtype=jnp.int32))
    finish = offset + lengths
    mine = row_owner == group
    places = jnp.arange(total, dtype=jnp.int32)
    passed = mine[None, :] & (finish[None, :] <= places[:, None])
    return lax.optimization_barrier(jnp.sum(passed.astype(jnp.int32), axis=1, dtype=jnp.int32))

def block_links(segments):
    blocks = segments.reshape(-1, BLOCK)
    links = (blocks[1:, 0] == blocks[:-1, -1]).astype(jnp.float32)
    return (blocks, jnp.concatenate([jnp.zeros((1,), jnp.float32), links]))

def head_attention(query, key, value, blocks, links):
    width = value.shape[-1]
    feats = 1 + query.shape[-1] + query.shape[-1] * query.shape[-1]
    places = jnp.arange(BLOCK)
    causal = places[:, None] >= places[None, :]

    def advance(carry, inputs):
        state, norm_sum = carry
        query_block, key_block, value_block, segment_block, link = inputs
        state = state * link
        norm_sum = norm_sum * link
        scores = low_back(matmul(query_block, key_block.T) / math.sqrt(query_block.shape[-1]))
        mask = causal & (segment_block[:, None] == segment_block[None, :])
        kernel = jnp.where(mask, 1.0 + scores + 0.5 * scores * scores, 0.0)
        query_feats = taylor_features(query_block)
        key_feats = low(taylor_features(key_block))
        weighted = matmul(low(kernel), value_block) + matmul(low(query_feats).T, low(state))
        weight_total = lax.optimization_barrier(jnp.sum(kernel, axis=1)) + matmul(norm_sum, query_feats)
        weighted = low_back(weighted)
        result = low(weighted / weight_total[:, None])
        increment = low_back(matmul(key_feats, value_block))
        return ((state + increment, norm_sum + lax.optimization_barrier(jnp.sum(key_feats, axis=1))), result)
    start = (jnp.zeros((feats, width), jnp.float32), jnp.zeros((feats,), jnp.float32))
    _, results = lax.scan(jax.checkpoint(advance), start, (query, key, value, blocks, links))
    return results

def attention(query, key, value, segments):
    total = query.shape[0]
    count = total // BLOCK

    def split_heads(values, width):
        return values.reshape(count, BLOCK, -1, width).transpose(2, 0, 1, 3)
    blocks, links = block_links(segments)
    results = jax.vmap(head_attention, in_axes=(0, 0, 0, None, None))(split_heads(query, FEAT), split_heads(key, FEAT), split_heads(value, HV), blocks, links)
    return results.transpose(1, 2, 0, 3).reshape(total, -1)

def layer(rows_in, segments, weights):
    gain_first, w_query, w_key, w_value, w_out, gain_second, w_gate, w_up, w_down = weights
    normed = low(root_norm(rows_in, gain_first))
    query = low_back(low(matmul(normed, w_query)))
    key = low_back(low(matmul(normed, w_key)))
    value = low_back(low(matmul(normed, w_value)))
    mixed = attention(query, key, value, segments)
    middle = rows_in + low_back(matmul(mixed, w_out))
    normed_second = low(root_norm(middle, gain_second))
    gate = low_back(matmul(normed_second, w_gate))
    upward = low_back(matmul(normed_second, w_up))
    hidden = low(jax.nn.silu(gate) * upward)
    return middle + low_back(matmul(hidden, w_down))

def reference(layer_input, lengths, row_owner, norm_gain1, w_query, w_key, w_value, w_out, norm_gain2, w_gate, w_up, w_down, cotangent):
    weights = (norm_gain1.astype(jnp.float32), w_query.astype(jnp.float32), w_key.astype(jnp.float32), w_value.astype(jnp.float32), w_out.astype(jnp.float32), norm_gain2.astype(jnp.float32), w_gate.astype(jnp.float32), w_up.astype(jnp.float32), w_down.astype(jnp.float32))
    groups = jnp.arange(N_DP, dtype=jnp.int32)
    segments_all = jax.vmap(lambda group: segment_numbers(lengths, row_owner, group, GROUP_TOK))(groups)
    rows_all = layer_input.reshape(N_DP, GROUP_TOK, D)
    grads_all = cotangent.reshape(N_DP, GROUP_TOK, D)

    def one_group(totals, inputs):
        rows_in, grad_rows, segments = inputs
        result, pullback = jax.vjp(lambda rows, params: layer(rows, segments, params), rows_in, weights)
        grad_input, grad_weights = pullback(grad_rows)
        return (jax.tree.map(lambda first, second: first + second, totals, grad_weights), (result, grad_input))
    zeros = jax.tree.map(jnp.zeros_like, weights)
    grads, (results, input_grads) = lax.scan(one_group, zeros, (rows_all, grads_all, segments_all))
    return (results.reshape(TOKENS, D), input_grads.reshape(TOKENS, D), grads[0], grads[1], grads[2], grads[3], grads[4], grads[5], grads[6], grads[7], grads[8])
```

```python
import math

import jax
import jax.numpy as jnp
from jax import lax
from jax.experimental import pallas as pl
from jax.experimental.pallas import tpu as pltpu
from jax.sharding import PartitionSpec as P

FEAT = 16
HV = 128
BLOCK = 512


EPS = 1e-05
HIGHEST = lax.Precision.HIGHEST
CONTRACT_FIRST = (((0,), (0,)), ((), ()))
CONTRACT_LAST = (((1,), (1,)), ((), ()))


def root_scale(values):
    return lax.rsqrt(jnp.mean(values * values, axis=-1, keepdims=True) + EPS)


def norm_back(grad, values, scale):
    return scale * grad - values * scale**3 * jnp.mean(grad * values, axis=-1, keepdims=True)


def taylor_features(rows):
    columns = rows.T
    width = columns.shape[0]
    outer = (columns[:, None, :] * columns[None, :, :]).reshape(width * width, columns.shape[1])
    ones = jnp.ones((1, columns.shape[1]), columns.dtype)
    return jnp.concatenate(
        [ones, columns / math.sqrt(math.sqrt(width)), outer / (math.sqrt(2.0) * math.sqrt(width))],
        axis=0,
    )


def segment_numbers(lengths, row_owner, group, total):
    order = jnp.arange(lengths.shape[0], dtype=jnp.int32)
    same = row_owner[:, None] == row_owner[None, :]
    before = same & (order[None, :] < order[:, None])
    offset = jnp.sum(jnp.where(before, lengths[None, :], 0), axis=1, dtype=jnp.int32)
    finish = offset + lengths
    mine = row_owner == group
    places = jnp.arange(total, dtype=jnp.int32)
    passed = mine[None, :] & (finish[None, :] <= places[:, None])
    return jnp.sum(passed.astype(jnp.int32), axis=1, dtype=jnp.int32)


def block_links(segments):
    blocks = segments.reshape(-1, BLOCK)
    links = (blocks[1:, 0] == blocks[:-1, -1]).astype(jnp.float32)
    return (blocks, jnp.concatenate([jnp.zeros((1,), jnp.float32), links]))


def causal_mask(segment_block):
    places = jnp.arange(segment_block.shape[0])
    return (places[:, None] >= places[None, :]) & (segment_block[:, None] == segment_block[None, :])


def kernel_scores(query_block, key_block, mask):
    scores = jnp.dot(query_block, key_block.T, preferred_element_type=jnp.float32) / math.sqrt(
        query_block.shape[-1]
    )
    kernel = jnp.where(mask, 1.0 + scores + 0.5 * scores * scores, 0.0)
    return (scores, kernel)


def head_forward(query_head, key_head, value_head, segment_blocks, links):
    feats = 1 + FEAT + FEAT * FEAT
    width = value_head.shape[-1]

    def advance(carry, inputs):
        state, norm_sum = carry
        query_block, key_block, value_block, segment_block, link = inputs
        state = state * link
        norm_sum = norm_sum * link
        mask = causal_mask(segment_block)
        scores, kernel = kernel_scores(query_block, key_block, mask)
        query_feats = taylor_features(query_block.astype(jnp.float32))
        key_feats = taylor_features(key_block.astype(jnp.float32)).astype(jnp.bfloat16)
        weighted = jnp.dot(
            kernel.astype(jnp.bfloat16), value_block, preferred_element_type=jnp.float32
        )
        weighted = weighted + lax.dot_general(
            query_feats.astype(jnp.bfloat16),
            state.astype(jnp.bfloat16),
            CONTRACT_FIRST,
            preferred_element_type=jnp.float32,
        )
        weight_total = jnp.sum(kernel, axis=1) + jnp.dot(norm_sum, query_feats, precision=HIGHEST)
        ratio = weighted / weight_total[:, None]
        new_state = state + jnp.dot(key_feats, value_block, preferred_element_type=jnp.float32)
        new_norm = norm_sum + jnp.sum(key_feats.astype(jnp.float32), axis=1)
        return ((new_state, new_norm), (ratio, weight_total, state, norm_sum))

    start = (jnp.zeros((feats, width), jnp.float32), jnp.zeros((feats,), jnp.float32))
    _, kept = lax.scan(advance, start, (query_head, key_head, value_head, segment_blocks, links))
    return kept


def head_backward(
    query_head,
    key_head,
    value_head,
    segment_blocks,
    links,
    states,
    norms,
    grad_weighted,
    grad_total,
):
    feats = 1 + FEAT + FEAT * FEAT
    width = value_head.shape[-1]

    def retreat(carry, inputs):
        grad_state, grad_norm = carry
        (
            query_block,
            key_block,
            value_block,
            segment_block,
            link,
            state,
            norm_sum,
            grad_block,
            grad_sum,
        ) = inputs
        mask = causal_mask(segment_block)
        scores, kernel = kernel_scores(query_block, key_block, mask)
        query_feats, query_pull = jax.vjp(taylor_features, query_block.astype(jnp.float32))
        key_exact, key_pull = jax.vjp(taylor_features, key_block.astype(jnp.float32))
        key_feats = key_exact.astype(jnp.bfloat16)
        query_low = query_feats.astype(jnp.bfloat16)
        state_low = state.astype(jnp.bfloat16)
        carry_low = grad_state.astype(jnp.bfloat16)
        grad_kernel = (
            jnp.dot(grad_block, value_block.T, preferred_element_type=jnp.float32)
            + grad_sum[:, None]
        )
        grad_scores = jnp.where(mask, grad_kernel * (1.0 + scores), 0.0).astype(jnp.bfloat16)
        divisor = math.sqrt(query_block.shape[-1])
        grad_query = jnp.dot(grad_scores, key_block, preferred_element_type=jnp.float32) / divisor
        grad_key = jnp.dot(grad_scores.T, query_block, preferred_element_type=jnp.float32) / divisor
        grad_value = jnp.dot(
            kernel.astype(jnp.bfloat16).T, grad_block, preferred_element_type=jnp.float32
        )
        grad_value = grad_value + lax.dot_general(
            key_feats, carry_low, CONTRACT_FIRST, preferred_element_type=jnp.float32
        )
        grad_query_feats = (
            jnp.dot(state_low, grad_block.T, preferred_element_type=jnp.float32)
            + norm_sum[:, None] * grad_sum[None, :]
        )
        grad_key_feats = (
            jnp.dot(carry_low, value_block.T, preferred_element_type=jnp.float32)
            + grad_norm[:, None]
        )
        grad_query = grad_query + query_pull(grad_query_feats)[0]
        grad_key = grad_key + key_pull(grad_key_feats)[0]
        back_state = (
            grad_state + jnp.dot(query_low, grad_block, preferred_element_type=jnp.float32)
        ) * link
        back_norm = (grad_norm + jnp.dot(query_feats, grad_sum, precision=HIGHEST)) * link
        return (
            (back_state, back_norm),
            (
                grad_query.astype(jnp.bfloat16),
                grad_key.astype(jnp.bfloat16),
                grad_value.astype(jnp.bfloat16),
            ),
        )

    start = (jnp.zeros((feats, width), jnp.float32), jnp.zeros((feats,), jnp.float32))
    _, grads = lax.scan(
        retreat,
        start,
        (
            query_head,
            key_head,
            value_head,
            segment_blocks,
            links,
            states,
            norms,
            grad_weighted,
            grad_total,
        ),
        reverse=True,
    )
    return grads


def on_device(
    layer_input,
    lengths,
    row_owner,
    norm_gain1,
    w_query,
    w_key,
    w_value,
    w_out,
    norm_gain2,
    w_gate,
    w_up,
    w_down,
    cotangent,
):
    parts = lax.axis_size("tp")
    group = lax.axis_index("dp")
    local_rows = layer_input.shape[0]
    group_rows = local_rows * parts
    blocks = group_rows // BLOCK
    segments = segment_numbers(lengths, row_owner, group, group_rows)
    segment_blocks, links = block_links(segments)

    def split_heads(values, width):
        return values.reshape(blocks, BLOCK, -1, width).transpose(2, 0, 1, 3)

    def merge_heads(values):
        return values.transpose(1, 2, 0, 3).reshape(group_rows, -1)

    scale_first = root_scale(layer_input)
    normed_first = (layer_input * scale_first * norm_gain1).astype(jnp.bfloat16)
    gathered_first = lax.all_gather(normed_first, "tp", axis=0, tiled=True)
    query = jnp.dot(gathered_first, w_query, preferred_element_type=jnp.float32).astype(
        jnp.bfloat16
    )
    key = jnp.dot(gathered_first, w_key, preferred_element_type=jnp.float32).astype(jnp.bfloat16)
    value = jnp.dot(gathered_first, w_value, preferred_element_type=jnp.float32).astype(
        jnp.bfloat16
    )
    query_heads = split_heads(query, FEAT)
    key_heads = split_heads(key, FEAT)
    value_heads = split_heads(value, HV)
    ratio, totals, states, norms = jax.vmap(head_forward, in_axes=(0, 0, 0, None, None))(
        query_heads, key_heads, value_heads, segment_blocks, links
    )
    mixed = merge_heads(ratio).astype(jnp.bfloat16)
    attended = lax.psum_scatter(
        jnp.dot(mixed, w_out, preferred_element_type=jnp.float32),
        "tp",
        scatter_dimension=0,
        tiled=True,
    )
    middle = layer_input + attended
    scale_second = root_scale(middle)
    normed_second = (middle * scale_second * norm_gain2).astype(jnp.bfloat16)
    gathered_second = lax.all_gather(normed_second, "tp", axis=0, tiled=True)
    gate = jnp.dot(gathered_second, w_gate, preferred_element_type=jnp.float32)
    upward = jnp.dot(gathered_second, w_up, preferred_element_type=jnp.float32)
    sigmoid = jax.nn.sigmoid(gate)
    activated = gate * sigmoid
    hidden = (activated * upward).astype(jnp.bfloat16)
    output = middle + lax.psum_scatter(
        jnp.dot(hidden, w_down, preferred_element_type=jnp.float32).astype(jnp.bfloat16),
        "tp",
        scatter_dimension=0,
        tiled=True,
    ).astype(jnp.float32)
    top_rows = lax.all_gather(cotangent.astype(jnp.bfloat16), "tp", axis=0, tiled=True)
    grad_hidden = lax.dot_general(
        top_rows, w_down, CONTRACT_LAST, preferred_element_type=jnp.float32
    )
    grad_down = lax.dot_general(
        hidden, top_rows, CONTRACT_FIRST, preferred_element_type=jnp.float32
    )
    grad_gate_rows = (grad_hidden * upward * sigmoid * (1.0 + gate * (1.0 - sigmoid))).astype(
        jnp.bfloat16
    )
    grad_up_rows = (grad_hidden * activated).astype(jnp.bfloat16)
    grad_gate = lax.dot_general(
        gathered_second, grad_gate_rows, CONTRACT_FIRST, preferred_element_type=jnp.float32
    )
    grad_up = lax.dot_general(
        gathered_second, grad_up_rows, CONTRACT_FIRST, preferred_element_type=jnp.float32
    )
    grad_normed_second = lax.psum_scatter(
        lax.dot_general(grad_gate_rows, w_gate, CONTRACT_LAST, preferred_element_type=jnp.float32)
        + lax.dot_general(grad_up_rows, w_up, CONTRACT_LAST, preferred_element_type=jnp.float32),
        "tp",
        scatter_dimension=0,
        tiled=True,
    )
    gain_second_part = jnp.sum(grad_normed_second * middle * scale_second, axis=0)
    grad_middle = cotangent + norm_back(grad_normed_second * norm_gain2, middle, scale_second)
    grad_middle_low = grad_middle.astype(jnp.bfloat16)
    middle_rows = lax.all_gather(grad_middle_low, "tp", axis=0, tiled=True)
    grad_mixed = lax.dot_general(
        middle_rows, w_out, CONTRACT_LAST, preferred_element_type=jnp.float32
    )
    grad_out = lax.dot_general(
        mixed, middle_rows, CONTRACT_FIRST, preferred_element_type=jnp.float32
    )
    grad_ratio = split_heads(grad_mixed, HV)
    grad_weighted = (grad_ratio / totals[..., None]).astype(jnp.bfloat16)
    grad_total = -jnp.sum(grad_ratio * ratio, axis=-1) / totals
    head_grads = jax.vmap(head_backward, in_axes=(0, 0, 0, None, None, 0, 0, 0, 0))
    grad_query_heads, grad_key_heads, grad_value_heads = head_grads(
        query_heads,
        key_heads,
        value_heads,
        segment_blocks,
        links,
        states,
        norms,
        grad_weighted,
        grad_total,
    )
    grad_query_rows = merge_heads(grad_query_heads)
    grad_key_rows = merge_heads(grad_key_heads)
    grad_value_rows = merge_heads(grad_value_heads)
    grad_query = lax.dot_general(
        gathered_first, grad_query_rows, CONTRACT_FIRST, preferred_element_type=jnp.float32
    )
    grad_key = lax.dot_general(
        gathered_first, grad_key_rows, CONTRACT_FIRST, preferred_element_type=jnp.float32
    )
    grad_value = lax.dot_general(
        gathered_first, grad_value_rows, CONTRACT_FIRST, preferred_element_type=jnp.float32
    )
    result = lax.dot_general(
        grad_query_rows, w_query, CONTRACT_LAST, preferred_element_type=jnp.float32
    )
    result = result + lax.dot_general(
        grad_key_rows, w_key, CONTRACT_LAST, preferred_element_type=jnp.float32
    )
    grad_normed_first = lax.psum_scatter(
        (
            result
            + lax.dot_general(
                grad_value_rows, w_value, CONTRACT_LAST, preferred_element_type=jnp.float32
            )
        ).astype(jnp.bfloat16),
        "tp",
        scatter_dimension=0,
        tiled=True,
    ).astype(jnp.float32)
    gain_first_part = jnp.sum(grad_normed_first * layer_input * scale_first, axis=0)
    input_grad = grad_middle + norm_back(grad_normed_first * norm_gain1, layer_input, scale_first)
    gain_first, gain_second = lax.psum((gain_first_part, gain_second_part), ("dp", "tp"))
    summed = (
        lax.psum_scatter(
            grad_query.astype(jnp.bfloat16), "dp", scatter_dimension=0, tiled=True
        ).astype(jnp.float32),
        lax.psum_scatter(
            grad_key.astype(jnp.bfloat16), "dp", scatter_dimension=0, tiled=True
        ).astype(jnp.float32),
        lax.psum_scatter(
            grad_value.astype(jnp.bfloat16), "dp", scatter_dimension=0, tiled=True
        ).astype(jnp.float32),
        lax.psum_scatter(
            grad_out.astype(jnp.bfloat16), "dp", scatter_dimension=1, tiled=True
        ).astype(jnp.float32),
        lax.psum_scatter(
            grad_gate.astype(jnp.bfloat16), "dp", scatter_dimension=0, tiled=True
        ).astype(jnp.float32),
        lax.psum_scatter(
            grad_up.astype(jnp.bfloat16), "dp", scatter_dimension=0, tiled=True
        ).astype(jnp.float32),
        lax.psum_scatter(
            grad_down.astype(jnp.bfloat16), "dp", scatter_dimension=1, tiled=True
        ).astype(jnp.float32),
    )
    return (
        output,
        input_grad,
        gain_first,
        summed[0],
        summed[1],
        summed[2],
        summed[3],
        gain_second,
        summed[4],
        summed[5],
        summed[6],
    )


QUADS = FEAT // 2 + 1
FEATS = (QUADS + 2) * FEAT
HALF_TURN = 1.0 / math.sqrt(2.0 * FEAT)
PAIR_TURN = 1.0 / math.sqrt(1.0 * FEAT)
LINE = 1.0 / math.sqrt(math.sqrt(FEAT))
SHRINK = 1.0 / math.sqrt(FEAT)
NT = (((1,), (1,)), ((), ()))
TN = (((0,), (0,)), ((), ()))
NN = (((1,), (0,)), ((), ()))


def mm(left, right, dims=NN):
    return lax.dot_general(left, right, dims, preferred_element_type=jnp.float32)


def quad_scale(shift):
    return HALF_TURN if shift in (0, FEAT // 2) else PAIR_TURN


def features(u):
    rows = [u * u * HALF_TURN]
    for shift in range(1, QUADS):
        rows.append(u * pltpu.roll(u, shift, 0) * quad_scale(shift))
    first = lax.broadcasted_iota(jnp.int32, u.shape, 0) == 0
    rows.append(u * LINE)
    rows.append(jnp.where(first, 1.0, 0.0))
    return jnp.concatenate(rows, axis=0)


def features_back(u, grad):
    total = 2.0 * HALF_TURN * u * grad[:FEAT] + LINE * grad[QUADS * FEAT : (QUADS + 1) * FEAT]
    for shift in range(1, QUADS):
        part = grad[shift * FEAT : (shift + 1) * FEAT]
        both = pltpu.roll(u, shift, 0) * part + pltpu.roll(u * part, FEAT - shift, 0)
        total = total + quad_scale(shift) * both
    return total


def with_ones(value):
    return jnp.concatenate([value, jnp.ones(value.shape, value.dtype)], axis=1)


def row_to_columns(row):
    tall = jnp.broadcast_to(row, (HV, row.shape[1]))
    return tall.T[:FEATS]


def increment_kernel(key_ref, value_ref, state_ref, norm_ref):
    feats = features(key_ref[...].astype(jnp.float32)).astype(jnp.bfloat16)
    state_ref[0] = mm(feats, value_ref[...]).astype(jnp.bfloat16)
    row = mm(jnp.ones((16, feats.shape[1]), jnp.bfloat16), feats, NT)[:1]
    norm_ref[0] = jnp.concatenate([row, jnp.zeros((1, 256 - FEATS), jnp.float32)], axis=1)


def local_kernel(query_ref, key_ref, value_ref, sums_ref):
    query = query_ref[...]
    scores = mm(query.astype(jnp.float32).T.astype(jnp.bfloat16), key_ref[...]) * SHRINK
    rows = lax.broadcasted_iota(jnp.int32, scores.shape, 0)
    cols = lax.broadcasted_iota(jnp.int32, scores.shape, 1)
    kernel = jnp.where(rows >= cols, 1.0 + scores + 0.5 * scores * scores, 0.0)
    sums_ref[...] = mm(kernel.astype(jnp.bfloat16), with_ones(value_ref[...]))


def joined(weight_ref, states, norms):
    state = jnp.zeros((FEATS, HV), jnp.float32)
    norm = jnp.zeros((1, 256), jnp.float32)
    for place in range(len(states)):
        keep = weight_ref[1 + place] != 0
        state = state + jnp.where(keep, states[place][0].astype(jnp.float32), 0.0)
        norm = norm + jnp.where(keep, norms[place][0], 0.0)
    return state, norm


def combine_kernel(weight_ref, query_ref, sums_ref, s1, s2, s3, m1, m2, m3, mixed_ref, total_ref, all_ref):
    state, norm = joined(weight_ref, (s1, s2, s3), (m1, m2, m3))
    both = jnp.concatenate([state, row_to_columns(norm)], axis=1).astype(jnp.bfloat16)
    all_ref[0] = both
    feats = features(query_ref[...].astype(jnp.float32))
    sums = sums_ref[...] + mm(feats.T.astype(jnp.bfloat16), both)
    total = sums[:, HV:]
    mixed_ref[...] = (sums[:, :HV] / total).astype(jnp.bfloat16)
    total_ref[...] = total


def carry_kernel(weight_ref, query_ref, grad_ref, total_ref, mixed_ref, pulled_ref, carry_ref, norm_ref):
    grad, total = grad_ref[...], total_ref[...]
    pulled = (grad / total).astype(jnp.bfloat16)
    along = -jnp.sum(grad * mixed_ref[...].astype(jnp.float32), axis=1, keepdims=True) / total
    low = (along * (1.0 / HV)).astype(jnp.bfloat16)
    pulled_ref[...] = jnp.concatenate([pulled, low], axis=1)
    feats = features(query_ref[...].astype(jnp.float32)).astype(jnp.bfloat16)
    carry_ref[0] = mm(feats, pulled).astype(jnp.bfloat16)
    turned = along.T[:16].astype(jnp.bfloat16)
    row = mm(turned, feats, NT)[:1]
    norm_ref[0] = jnp.concatenate([row, jnp.zeros((1, 256 - FEATS), jnp.float32)], axis=1)


def local_back_kernel(query_ref, key_ref, value_ref, pulled_ref, all_ref, grad_query_ref, grad_key_ref, grad_value_ref):
    query, key = query_ref[...], key_ref[...]
    value, pulled = with_ones(value_ref[...]), pulled_ref[...]
    scores = mm(key.astype(jnp.float32).T.astype(jnp.bfloat16), query) * SHRINK
    rows = lax.broadcasted_iota(jnp.int32, scores.shape, 0)
    cols = lax.broadcasted_iota(jnp.int32, scores.shape, 1)
    mask = cols >= rows
    kernel = jnp.where(mask, 1.0 + scores + 0.5 * scores * scores, 0.0).astype(jnp.bfloat16)
    grad_value_ref[...] = mm(kernel, pulled[:, :HV])
    grads = jnp.where(mask, mm(value, pulled, NT) * (1.0 + scores), 0.0).astype(jnp.bfloat16)
    grad_key_ref[...] = mm(query, grads, NT) * SHRINK
    grad_query = mm(key, grads) * SHRINK
    grad_feats = mm(all_ref[0], pulled, NT)
    grad_query_ref[...] = (
        grad_query + features_back(query.astype(jnp.float32), grad_feats)
    ).astype(jnp.bfloat16)


def combine_back_kernel(weight_ref, key_ref, value_ref, part_ref, gain_ref, s1, s2, s3, m1, m2, m3, grad_key_ref, grad_value_ref):
    carry, norm = joined(weight_ref, (s1, s2, s3), (m1, m2, m3))
    carry = carry.astype(jnp.bfloat16)
    key = key_ref[...].astype(jnp.float32)
    both = jnp.concatenate([carry, (row_to_columns(norm) * (1.0 / HV)).astype(jnp.bfloat16)], axis=1)
    grad_feats = mm(both, with_ones(value_ref[...]), NT)
    grad_key_ref[...] = (part_ref[...] + features_back(key, grad_feats)).astype(jnp.bfloat16)
    feats = features(key).astype(jnp.bfloat16).astype(jnp.float32)
    grad_value_ref[...] = (gain_ref[...] + mm(feats.T.astype(jnp.bfloat16), carry)).astype(jnp.bfloat16)


def head_call(kernel, heads, ins, outs, shapes, weights, operands, flops):
    spec = pltpu.PrefetchScalarGridSpec(
        num_scalar_prefetch=0 if weights is None else 1, grid=(heads,), in_specs=ins, out_specs=outs
    )
    moved = sum(v.size * v.dtype.itemsize for v in operands)
    moved += sum(math.prod(s.shape) * s.dtype.itemsize for s in shapes)
    call = pl.pallas_call(
        kernel,
        grid_spec=spec,
        out_shape=shapes,
        cost_estimate=pl.CostEstimate(flops=flops * heads, bytes_accessed=moved, transcendentals=0),
        compiler_params=pltpu.CompilerParams(dimension_semantics=("arbitrary",)),
    )
    return call(*operands) if weights is None else call(weights, *operands)


def pick_specs(rows, heads, per):
    query = pl.BlockSpec((FEAT, rows), lambda h, *_: (h, 0))
    key = pl.BlockSpec((FEAT, rows), lambda h, *_: (heads + h, 0))
    value = pl.BlockSpec((rows, HV), lambda h, *_: (0, h))
    wide = pl.BlockSpec((rows, 2 * HV), lambda h, *_: (0, h))
    state = pl.BlockSpec((1, FEATS, HV), lambda h, *_: (h, 0, 0))
    norm = pl.BlockSpec((1, 1, 256), lambda h, *_: (h, 0, 0))
    both = pl.BlockSpec((1, FEATS, 2 * HV), lambda h, *_: (h, 0, 0))

    def shuffled(h, weights):
        part, place = h // per, h % per
        pair = place // (per // 2)
        other = jnp.where(pair == weights[0], 0, 1)
        return (0, other * (heads // 2) + part * (per // 2) + place % (per // 2))

    mixed = pl.BlockSpec((rows, HV), shuffled)
    def seen(block, shift):
        return pl.BlockSpec(block, lambda h, *_: (((h // per) ^ shift) * per + h % per, 0, 0))

    others = [seen((1, FEATS, HV), s) for s in (1, 2, 3)] + [seen((1, 1, 256), s) for s in (1, 2, 3)]
    return query, key, value, wide, state, norm, both, mixed, others


def hop(value, shift):
    return lax.ppermute(value, "tp", [(i, i ^ shift) for i in range(4)])


def later(value, shift):
    return lax.ppermute(value, "tp", [(i, i ^ shift) for i in range(4) if i < i ^ shift])


def earlier(value, shift):
    return lax.ppermute(value, "tp", [(i, i ^ shift) for i in range(4) if i > i ^ shift])


def swap(value):
    size = lax.axis_size("dp")
    return lax.ppermute(value, "dp", [(i, i ^ 1) for i in range(size)])


def spread(value):
    half = value.shape[0] // 2
    across, along = hop(value, 1), hop(value, 2)
    return value, across, along, hop(across[:half], 2), hop(along[half:], 1)


def collect(part):
    low = lambda v: v.astype(jnp.bfloat16)
    wide = lambda v: v.astype(jnp.float32)
    sent_a, sent_b = hop(low(part(3, 0)), 1), hop(low(part(3, 1)), 2)
    x_a = hop(low(part(1, 0)), 1)
    y_b = hop(low(part(2, 1)), 2)
    x_b = hop(low(part(1, 1) + wide(sent_b)), 1)
    y_a = hop(low(part(2, 0) + wide(sent_a)), 2)
    return (
        part(0, 0) + wide(x_a) + wide(y_a),
        part(0, 1) + wide(x_b) + wide(y_b),
    )


def z_sum(chunks):
    depth = lax.axis_size("dp") // 2
    place = lax.axis_index("dp") // 2
    total = chunks(place).astype(jnp.float32)
    for step in range(1, depth):
        away = [(i, (i + 2 * step) % (2 * depth)) for i in range(2 * depth)]
        got = lax.ppermute(chunks((place + step) % depth).astype(jnp.bfloat16), "dp", away)
        total = total + got.astype(jnp.float32)
    return total


def everywhere_sum(value):
    for shift in (1, 2):
        value = value + hop(value, shift)
    size = lax.axis_size("dp")
    shift = 1
    while shift < size:
        value = value + lax.ppermute(value, "dp", [(i, i ^ shift) for i in range(size)])
        shift *= 2
    return value


def by_block(layer_input, lengths, row_owner, norm_gain1, w_query, w_key, w_value, w_out, norm_gain2, w_gate, w_up, w_down, cotangent):
    bf = jnp.bfloat16
    f32 = jnp.float32
    group, here = lax.axis_index("dp"), lax.axis_index("tp")
    core = group % 2
    rows, width = layer_input.shape
    per = w_value.shape[1] // HV
    heads = 4 * per
    half = width // 2
    segments = segment_numbers(lengths, row_owner, group, rows * 4)[:: rows]
    mine_segment = lax.dynamic_index_in_dim(segments, here, 0, False)
    others = jnp.stack([here ^ s for s in (1, 2, 3)])
    same = segments[others] == mine_segment
    before = jnp.concatenate([core[None], (same & (others < here)).astype(jnp.int32)])
    after = jnp.concatenate([core[None], (same & (others > here)).astype(jnp.int32)])

    def two(value, axis):
        size = value.shape[axis] // 2
        mine = lax.dynamic_slice_in_dim(value, core * size, size, axis)
        other = lax.dynamic_slice_in_dim(value, (1 - core) * size, size, axis)
        return mine, other

    def shared(mine, other):
        got = spread(mine)
        rest = [swap(v) for v in got[1:]]
        return got, (other, *rest)

    top = cotangent.astype(bf)
    packed = jnp.concatenate([w_query, w_key, w_value], axis=1)
    mine, other = two(packed, 0)
    pieces = shared(mine, other)
    narrow = per * FEAT

    def laid(columns):
        def row_of(got):
            own, across, along, far_a, far_b = [v[:, columns] for v in got]
            far = jnp.concatenate([far_a, far_b], axis=0)
            return jnp.concatenate([own, across, along, far], axis=1)
        return jnp.concatenate([row_of(p) for p in pieces], axis=0)

    all_value = laid(slice(2 * narrow, None))
    all_both = jnp.concatenate([laid(slice(0, narrow)), laid(slice(narrow, 2 * narrow))], axis=1)
    out_mine, out_other = two(w_out, 0)
    out_pieces = shared(out_mine, out_other)
    all_out = jnp.concatenate([v for p in out_pieces for v in p], axis=0)
    tops = spread(top)

    scale_first = root_scale(layer_input)
    normed_first = (layer_input * scale_first * norm_gain1).astype(bf)
    turned_first = jnp.concatenate(two(normed_first, 1), axis=1)
    both = lax.dot_general(all_both, turned_first, (((0,), (1,)), ((), ())), preferred_element_type=f32).astype(bf)
    value = mm(turned_first, all_value).astype(bf)

    query_s, key_s, value_s, wide_s, state_s, norm_s, both_s, mixed_s, others_s = pick_specs(rows, heads, per)
    shape = jax.ShapeDtypeStruct
    state_shape = shape((heads, FEATS, HV), bf)
    norm_shape = shape((heads, 1, 256), f32)
    dots = 2 * rows * rows
    state, norm = head_call(
        increment_kernel, heads, [key_s, value_s], [state_s, norm_s], [state_shape, norm_shape],
        None, (both, value), 2 * rows * 256 * 256)
    states = [later(state, s) for s in (1, 2, 3)]
    norms = [later(norm, s) for s in (1, 2, 3)]
    sums = head_call(
        local_kernel, heads, [query_s, key_s, value_s], [wide_s], [shape((rows, heads * 2 * HV), f32)],
        None, (both, both, value), dots * 512)[0]
    mixed, total, joint = head_call(
        combine_kernel, heads, [query_s, wide_s] + others_s, [mixed_s, value_s, both_s],
        [shape((rows, heads * HV), bf), shape((rows, heads * HV), f32), shape((heads, FEATS, 2 * HV), bf)],
        before, (both, sums, *states, *norms), 2 * rows * 256 * 256)
    middle = layer_input + mm(mixed, all_out)
    scale_second = root_scale(middle)
    normed_second = (middle * scale_second * norm_gain2).astype(bf)
    seconds = spread(normed_second)

    def gathered(got):
        return [got[0], got[1], got[2], jnp.concatenate([got[3], got[4]], axis=0)]

    seconds, tops = gathered(seconds), gathered(tops)
    hiddens, gates, ups, outs, backs = [], [], [], [], []
    for rho in range(4):
        gate, up = mm(seconds[rho], w_gate), mm(seconds[rho], w_up)
        sigmoid = jax.nn.sigmoid(gate)
        activated = gate * sigmoid
        hidden = (activated * up).astype(bf)
        grad_hidden = mm(tops[rho], w_down, NT)
        grad_gate = (grad_hidden * up * sigmoid * (1.0 + gate * (1.0 - sigmoid))).astype(bf)
        grad_up = (grad_hidden * activated).astype(bf)
        hiddens.append(hidden)
        gates.append(grad_gate)
        ups.append(grad_up)
        outs.append(mm(hidden, w_down))
        backs.append(mm(grad_gate, w_gate, NT) + mm(grad_up, w_up, NT))
    part_of = lambda parts: lambda rho, side: parts[rho][side * (rows // 2) : (side + 1) * (rows // 2)]
    grad_normed_second = jnp.concatenate(collect(part_of(backs)), axis=0)
    gain_second_part = jnp.sum(grad_normed_second * middle * scale_second, axis=0)
    grad_middle = cotangent + norm_back(grad_normed_second * norm_gain2, middle, scale_second)
    grad_middle_low = grad_middle.astype(bf)
    grad_mixed = mm(grad_middle_low, all_out, NT)
    pulled, carry, carry_norm = head_call(
        carry_kernel, heads, [query_s, mixed_s, value_s, mixed_s], [wide_s, state_s, norm_s],
        [shape((rows, heads * 2 * HV), bf), state_shape, norm_shape],
        before, (both, grad_mixed, total, mixed), 2 * rows * 256 * 256)
    carries = [earlier(carry, s) for s in (1, 2, 3)]
    carry_norms = [earlier(carry_norm, s) for s in (1, 2, 3)]
    thin_s = pl.BlockSpec((FEAT, rows), lambda h, *_: (h, 0))
    thin = (heads * FEAT, rows)
    grad_query, key_part, value_part = head_call(
        local_back_kernel, heads, [query_s, key_s, value_s, wide_s, both_s], [thin_s, thin_s, value_s],
        [shape(thin, bf), shape(thin, f32), shape((rows, heads * HV), f32)],
        None, (both, both, value, pulled, joint), dots * 1024)
    grad_key, grad_value = head_call(
        combine_back_kernel, heads, [key_s, value_s, thin_s, value_s] + others_s, [thin_s, value_s],
        [shape(thin, bf), shape((rows, heads * HV), bf)],
        after, (both, value, key_part, value_part, *carries, *carry_norms), 4 * rows * 256 * 256)
    grad_both = jnp.concatenate([grad_query, grad_key], axis=0)
    turned_back = lax.dot_general(grad_both, all_both, (((0,), (1,)), ((), ())), preferred_element_type=f32)
    turned_back = turned_back + mm(grad_value, all_value, NT)
    grad_normed_first = jnp.where(
        core == 0, turned_back, jnp.concatenate([turned_back[:, half:], turned_back[:, :half]], axis=1))
    gain_first_part = jnp.sum(grad_normed_first * layer_input * scale_first, axis=0)
    input_grad = grad_middle + norm_back(grad_normed_first * norm_gain1, layer_input, scale_first)
    gains = everywhere_sum(jnp.stack([gain_first_part, gain_second_part]))

    second_all = jnp.concatenate(seconds, axis=0)
    top_all = jnp.concatenate(tops, axis=0)
    hidden_all = jnp.concatenate(hiddens, axis=0)
    down_part = mm(hidden_all, top_all, TN).astype(bf)
    gate_part = mm(second_all, jnp.concatenate(gates, axis=0), TN).astype(bf)
    up_part = mm(second_all, jnp.concatenate(ups, axis=0), TN).astype(bf)
    scatter = lambda v, axis: lax.psum_scatter(v, "dp", scatter_dimension=axis, tiled=True).astype(f32)
    down_grad, gate_grad, up_grad = scatter(down_part, 1), scatter(gate_part, 0), scatter(up_part, 0)
    output = middle + jnp.concatenate(collect(part_of(outs)), axis=0)

    depth = lax.axis_size("dp") // 2
    piece = width // (2 * depth)

    def by_core(value):
        split = value.reshape(rows, depth, 2, piece)
        pick = lambda at: lax.dynamic_index_in_dim(split, at, 2, False).reshape(rows, depth * piece)
        return pick(core), pick(1 - core)

    low_mine, low_other = by_core(grad_middle_low)
    got = swap(mm(mixed, low_other, TN).astype(bf)).astype(f32)
    got = jnp.concatenate([got[half:], got[:half]], axis=0)
    out_sum = mm(mixed, low_mine, TN) + got
    pair = per // 2 * HV
    out_part = lambda rho, side: out_sum[side * half + rho * pair : side * half + (rho + 1) * pair]
    out_half = collect(out_part)
    out_chunks = jnp.concatenate(out_half, axis=0)
    out_own = z_sum(lambda k: lax.dynamic_slice_in_dim(out_chunks, k * piece, piece, 1))
    out_grad = jnp.where(core == 0, out_own, jnp.concatenate([out_own[pair:], out_own[:pair]], axis=0))

    first_mine, first_other = by_core(normed_first)
    got_value = swap(mm(first_other, grad_value, TN).astype(bf)).astype(f32)
    got_both = swap(mm(first_other, grad_both, (((0,), (1,)), ((), ()))).astype(bf)).astype(f32)
    value_sum = mm(first_mine, grad_value, TN) + got_value
    both_sum = mm(first_mine, grad_both, (((0,), (1,)), ((), ()))) + got_both

    def first_part(rho, side):
        take = slice(side * (half // 2), (side + 1) * (half // 2))
        return jnp.concatenate(
            [
                both_sum[take, rho * narrow : (rho + 1) * narrow],
                both_sum[take, heads * FEAT + rho * narrow : heads * FEAT + (rho + 1) * narrow],
                value_sum[take, rho * per * HV : (rho + 1) * per * HV],
            ],
            axis=1,
        )

    chunks = jnp.concatenate(collect(first_part), axis=0)
    own = z_sum(lambda k: lax.dynamic_slice_in_dim(chunks, k * piece, piece, 0))
    return (
        output,
        input_grad,
        gains[0],
        own[:, :narrow],
        own[:, narrow : 2 * narrow],
        own[:, 2 * narrow :],
        out_grad,
        gains[1],
        gate_grad,
        up_grad,
        down_grad,
    )


def fits(mesh):
    return mesh.shape["tp"] == 4 and mesh.shape["dp"] == 8


def solution(mesh):
    placed = (
        P(("dp", "tp"), None),
        P(),
        P(),
        P(),
        P(None, "tp"),
        P(None, "tp"),
        P(None, "tp"),
        P("tp", None),
        P(),
        P(None, "tp"),
        P(None, "tp"),
        P("tp", None),
        P(("dp", "tp"), None),
    )
    return jax.shard_map(
        by_block if fits(mesh) else on_device,
        mesh=mesh,
        in_specs=placed,
        out_specs=(
            P(("dp", "tp"), None),
            P(("dp", "tp"), None),
            P(),
            P("dp", "tp"),
            P("dp", "tp"),
            P("dp", "tp"),
            P("tp", "dp"),
            P(),
            P("dp", "tp"),
            P("dp", "tp"),
            P("tp", "dp"),
        ),
        check_vma=False,
    )
```
